32 devices in a mesh: groups: 2 (over y), sess: 2 (over core), ctx: 8 (over z, x).
Axes of the slice: x: 2, y: 2, z: 4, core: 2. Of those that a mesh axis runs over, the one named last changes fastest.
Arguments:
- queries: bfloat16 [4, 8, 4096], P(('groups', 'sess'), 'ctx'), parts along dimension 0, may hold values from -12 to 12
- new_kv: bfloat16 [4, 8, 1024], P(('groups', 'sess'), 'ctx'), parts along dimension 0, may hold values from -8 to 8
- kv_pool: bfloat16 [64, 128, 1024], P(('groups', 'sess', 'ctx')), parts along dimension 0, may hold values from -6 to 6
- page_ids: int32 [4, 8, 2], P('groups', 'ctx'), parts along dimension 0, may hold values from 0 to 3, as said below
- cached_lengths: int32 [4], P('groups'), parts along dimension 0, may hold values from 512 to 2048, as said below
Outputs:
- attended: bfloat16 [4, 8, 4096], P(('groups', 'sess'), 'ctx'), parts along dimension 0
The draws below stay inside these ranges and needn't reach their ends.
There are 2 independent parts, one for each index of `groups`. The reference program is written for one: setup_inputs(seed, part) draws one part's arguments, and reference() takes and returns one part's arrays. A program takes and returns all parts, laid end to end along the dimension named above; each array names one. Nothing has to cross between parts.
Inputs may be any that keep to these rules, and one draw needn't show every extreme that they name: For each context index c, the 4 entries page_ids[:, c, :] hold every number from 0 to 3 once; entry v names page v % 2 of the pool of session index v // 2 on the same context index. In some context index all pages of one session lie in the other session's pool. `cached_lengths`: some session has all 2048 positions cached.
All inputs are finite; a program needn't handle non-finite values.
Results may differ from the reference program's by a relative error of at most 0.0025.
Values may be sent and summed in bfloat16 or wider, within the bound.
No kernel may reach another device: no remote copies, remote signals or barrier semaphores. Data moves between devices by JAX's collectives and lax.ppermute only.
A program may use at most 64 MiB of HBM per device.

```python
import jax
import jax.numpy as jnp
from jax import lax

HQ = 32
KVH = 4
HD = 128
PAGE = 128
PAGES_DEV = 2
GROUP = 8
KVW = 1024
Q = 8
N_SESS = 2
N_CTX = 8


def page_table(key):
    base = jax.random.fold_in(key, 11)
    column_keys = jax.random.split(base, N_CTX)
    shuffled = jax.vmap(lambda column_key: jax.random.permutation(column_key, N_SESS * PAGES_DEV))(column_keys).astype(jnp.int32)
    special = jax.random.randint(jax.random.fold_in(base, 1), (), 0, N_CTX)
    flipped = jax.random.randint(jax.random.fold_in(base, 2), (), 0, 2)
    first_half = jax.random.permutation(jax.random.fold_in(base, 3), PAGES_DEV).astype(jnp.int32)
    second_half = jax.random.permutation(jax.random.fold_in(base, 4), PAGES_DEV).astype(jnp.int32)
    forced = jnp.concatenate([(1 - flipped) * PAGES_DEV + first_half, flipped * PAGES_DEV + second_half])
    columns = jnp.arange(N_CTX, dtype=jnp.int32)
    merged = jnp.where((columns == special)[:, None], forced[None, :], shuffled)
    return jnp.transpose(merged.reshape(N_CTX, N_SESS, PAGES_DEV), (1, 0, 2)).astype(jnp.int32)


def draw_page_ids(key, part):
    return page_table(key)


def draw_cached_lengths(key, part):
    base = jax.random.fold_in(key, 21)
    whole = PAGES_DEV * PAGE * N_CTX
    full_session = jax.random.randint(jax.random.fold_in(base, 1), (), 0, N_SESS)
    others = jax.random.randint(jax.random.fold_in(base, 2), (N_SESS,), whole // 4, whole + 1)
    sessions = jnp.arange(N_SESS, dtype=jnp.int32)
    return jnp.where(sessions == full_session, whole, others).astype(jnp.int32)


def draw_kv_pool(key, part):
    base = jax.random.fold_in(key, 41)
    pool_shape = (N_SESS * N_CTX * PAGES_DEV, PAGE, 2 * KVH * HD)
    values = jnp.clip(jax.random.normal(base, pool_shape, jnp.float32), -6.0, 6.0)
    return values.astype(jnp.bfloat16)


def draw_queries(key, part):
    base = jax.random.fold_in(key, 51)
    query_shape = (N_SESS, Q, HQ * HD)
    values = jnp.clip(3.0 * jax.random.normal(base, query_shape, jnp.float32), -12.0, 12.0)
    return values.astype(jnp.bfloat16)


def levels(stream_key, shape, shards, smallest, largest):
    loudness, own = 1.0, jax.random.fold_in(stream_key, 6)
    for axis_at, blocks in shards:
        steps = jnp.exp(jax.random.uniform(jax.random.fold_in(own, axis_at), (blocks,), jnp.float32, smallest / len(shards), largest / len(shards)))
        loudness = loudness * jnp.repeat(steps, shape[axis_at] // blocks).reshape([-1 if axis == axis_at else 1 for axis in range(len(shape))])
    return loudness


def normal_values(rng, extent, spread, reach, pieces=(), kind=jnp.bfloat16):
    factor_of = levels(rng, extent, pieces, -0.22, 0.18) if pieces else 1.0
    result = jax.random.normal(rng, extent, jnp.float32) * spread * factor_of
    return jnp.minimum(jnp.maximum(result, -reach), reach).astype(kind)


def setup_inputs(seed: int = 0, part: int = 0) -> dict:
    keys = jax.random.split(jax.random.key(seed), 6)
    part_keys = jax.random.split(jax.random.fold_in(keys[5], part), 6)
    return {
        "queries": draw_queries(jax.random.fold_in(jax.random.fold_in(keys[5], part), 71), part),
        "new_kv": normal_values(part_keys[1], (N_SESS, Q, KVW), 1.6, 8.0, ((0, 2), (1, 8))),
        "kv_pool": draw_kv_pool(jax.random.fold_in(jax.random.fold_in(keys[5], part), 71), part),
        "page_ids": draw_page_ids(jax.random.fold_in(jax.random.fold_in(keys[5], part), 71), part),
        "cached_lengths": draw_cached_lengths(jax.random.fold_in(jax.random.fold_in(keys[5], part), 71), part),
    }


masked_value = -1e30


def page_rows(page_ids, session):
    idents = page_ids[session]
    columns = jnp.arange(N_CTX, dtype=jnp.int32)[:, None]
    return ((idents // PAGES_DEV) * (N_CTX * PAGES_DEV) + columns * PAGES_DEV + idents % PAGES_DEV).astype(jnp.int32)


def column_block(kv_pool, pool_rows, column, query_heads, length):
    chosen = jnp.take(kv_pool, pool_rows[column], axis=0).reshape(PAGES_DEV * PAGE, 2, KVH, HD)
    scores = jnp.einsum("qkgd,rkd->qkgr", query_heads.astype(jnp.float32), chosen[:, 0].astype(jnp.float32)) * (HD ** -0.5)
    positions = column * (PAGES_DEV * PAGE) + jnp.arange(PAGES_DEV * PAGE, dtype=jnp.int32)
    scores = jnp.where((positions < length)[None, None, None, :], scores, masked_value)
    return scores, chosen[:, 1]


def one_session(query_block, fresh_kv, kv_pool, pool_rows, length):
    row_count = query_block.shape[0]
    query_heads = query_block.reshape(row_count, KVH, GROUP, HD)
    fresh_rows = fresh_kv.reshape(row_count, 2, KVH, HD)
    causal = jnp.arange(row_count, dtype=jnp.int32)[None, :] <= jnp.arange(row_count, dtype=jnp.int32)[:, None]
    fresh_scores = jnp.einsum("qkgd,rkd->qkgr", query_heads.astype(jnp.float32), fresh_rows[:, 0].astype(jnp.float32)) * (HD ** -0.5)
    fresh_scores = jnp.where(causal[:, None, None, :], fresh_scores, masked_value)

    def column_top(running, column):
        scores, unused = column_block(kv_pool, pool_rows, column, query_heads, length)
        return jnp.maximum(running, jnp.max(scores, axis=-1)), None

    row_top, unused = lax.scan(column_top, jnp.max(fresh_scores, axis=-1), jnp.arange(N_CTX, dtype=jnp.int32))

    def weigh(scores, values):
        weights = jnp.exp(scores - row_top[..., None])
        return jnp.sum(weights, axis=-1), jnp.einsum("qkgr,rkd->qkgd", weights, values.astype(jnp.float32))

    def column_sum(running_pair, column):
        weight_sum, summed = running_pair
        scores, values = column_block(kv_pool, pool_rows, column, query_heads, length)
        part_sum, part_vec = weigh(scores, values)
        return (weight_sum + part_sum, summed + part_vec), None

    initial = weigh(fresh_scores, fresh_rows[:, 1])
    (weight_sum, summed), unused = lax.scan(column_sum, initial, jnp.arange(N_CTX, dtype=jnp.int32))
    return (summed / weight_sum[..., None]).astype(jnp.bfloat16).reshape(row_count, -1)


def reference(queries, new_kv, kv_pool, page_ids, cached_lengths):
    outputs = [one_session(queries[session], new_kv[session], kv_pool, page_rows(page_ids, session), cached_lengths[session]) for session in range(N_SESS)]
    return jnp.stack(outputs)
```

```python
import functools

import jax
import jax.numpy as jnp
from jax import lax
from jax.experimental import pallas as pl
from jax.experimental.pallas import tpu as pltpu
from jax.sharding import PartitionSpec as P

KVH = 4
HD = 128
GROUP = 8
HQ = KVH * GROUP
STATE_ROWS = HQ + GROUP
masked_value = -1e30
GRANT = 2**24
VMEM = pltpu.VMEM
SMEM = pltpu.SMEM


def swapped(value, axis, mask):
    pairs = [(source, source ^ mask) for source in range(lax.axis_size(axis))]
    return lax.ppermute(value, axis, pairs)


def heads_kernel(own_ref, peer_ref, out_ref):
    for place, ref in enumerate((own_ref, peer_ref)):
        row = ref[0].astype(jnp.float32)
        out_ref[place * HQ : (place + 1) * HQ, :] = row.reshape(HQ, HD).astype(out_ref.dtype)


def join_kernel(own_ref, peer_ref, out_ref):
    rows = own_ref.shape[0]
    out_ref[:rows, :] = own_ref[...]
    out_ref[rows:, :] = peer_ref[...]


def pages_kernel(ids_ref, lengths_ref, pool_ref, peer_ref, cache_ref, bias_ref):
    session = lax.axis_index("sess")
    column = lax.axis_index("ctx")
    slots, page_len, _ = pool_ref.shape
    for slot in range(slots):
        ident = ids_ref[session, 0, slot]
        mine = (ident // slots) == session
        page = ident % slots
        cache_ref[slot * page_len : (slot + 1) * page_len, :] = jnp.where(
            mine, pool_ref[page], peer_ref[page]
        )
    rows = slots * page_len
    place = lax.broadcasted_iota(jnp.int32, bias_ref.shape, 1)
    left = lengths_ref[session] - column * rows
    bias_ref[...] = jnp.where(place < left, 0.0, masked_value)


def attend_kernel(own_ref, peer_ref, cache_ref, bias_ref, new_ref, out_ref):
    column = lax.axis_index("ctx")
    half = own_ref.shape[0] // HQ
    tokens = 2 * half
    own = own_ref[...].astype(jnp.float32)
    peer = peer_ref[...].astype(jnp.float32)
    bias = bias_ref[0:1, :]
    fresh = new_ref[0].astype(jnp.float32)
    place = lax.broadcasted_iota(jnp.int32, (GROUP, 1), 0)
    fresh_bias = jnp.concatenate(
        [jnp.where((place * 0 + (column ^ near)) >= column, 0.0, masked_value) for near in range(tokens)], axis=0
    )
    lane = lax.broadcasted_iota(jnp.int32, (tokens * GROUP, HD), 1)
    states = jnp.zeros((tokens * GROUP, HD), jnp.float32)
    for head in range(KVH):
        at = slice(head * HD, (head + 1) * HD)
        value_at = slice((KVH + head) * HD, (KVH + head + 1) * HD)
        query = jnp.concatenate(
            [
                part[near * HQ + head * GROUP : near * HQ + (head + 1) * GROUP]
                for part in (own, peer)
                for near in range(half)
            ],
            axis=0,
        )
        scores = lax.dot_general(
            query.astype(jnp.bfloat16), cache_ref[:, at], (((1,), (1,)), ((), ())),
            preferred_element_type=jnp.float32,
        )
        scores = scores * HD ** (-0.5) + bias
        fresh_scores = jnp.sum(query * fresh[:, at], axis=1, keepdims=True) * HD ** (-0.5) + fresh_bias
        top = jnp.maximum(jnp.max(scores, axis=1, keepdims=True), fresh_scores)
        weights = jnp.exp(scores - top)
        fresh_weights = jnp.exp(fresh_scores - top)
        total = jnp.sum(weights, axis=1, keepdims=True) + fresh_weights
        coarse = weights.astype(jnp.bfloat16)
        fine = (weights - coarse.astype(jnp.float32)).astype(jnp.bfloat16)
        values = cache_ref[:, value_at]
        summed = (
            jnp.dot(coarse, values, preferred_element_type=jnp.float32)
            + jnp.dot(fine, values, preferred_element_type=jnp.float32)
            + fresh_weights * fresh[:, value_at]
        )
        states = jnp.where(lane == head, top, states)
        states = jnp.where(lane == KVH + head, total, states)
        for near in range(tokens):
            out_ref[column ^ near, head * GROUP : (head + 1) * GROUP, :] = summed[near * GROUP : (near + 1) * GROUP]
    for near in range(tokens):
        out_ref[column ^ near, HQ:, :] = states[near * GROUP : (near + 1) * GROUP]


def settle_kernel(parts_ref, out_ref):
    devices = parts_ref.shape[0]
    tops = [parts_ref[source, HQ:, :] for source in range(devices)]
    highest = functools.reduce(jnp.maximum, tops)
    weight_sum = 0.0
    factors = []
    for states in tops:
        factor = jnp.exp(states - highest)
        factors.append(factor)
        weight_sum = weight_sum + pltpu.roll(states, HD - KVH, 1) * factor
    pieces = []
    for head in range(KVH):
        summed = 0.0
        for source in range(devices):
            summed = summed + parts_ref[source, head * GROUP : (head + 1) * GROUP, :] * factors[source][:, head : head + 1]
        pieces.append(summed / weight_sum[:, head : head + 1])
    result = jnp.concatenate(pieces, axis=0)
    out_ref[0] = result.reshape(1, HQ * HD).astype(out_ref.dtype)


def kernel_call(kernel, out_shape, in_spaces, *operands, name=None):
    shapes = out_shape if isinstance(out_shape, (tuple, list)) else (out_shape,)
    specs = [pl.BlockSpec(memory_space=VMEM) for _ in shapes]
    return pl.pallas_call(
        kernel,
        out_shape=out_shape,
        in_specs=[pl.BlockSpec(memory_space=space) for space in in_spaces],
        out_specs=specs if isinstance(out_shape, (tuple, list)) else specs[0],
        name=name,
        compiler_params=pltpu.CompilerParams(vmem_limit_bytes=GRANT),
    )(*operands)


def body(queries, new_kv, kv_pool, page_ids, cached_lengths):
    devices = lax.axis_size("ctx")
    shape = jax.ShapeDtypeStruct
    peer_queries = swapped(queries, "ctx", 1)
    peer_pool = swapped(kv_pool, "sess", 1)
    gathered = kernel_call(heads_kernel, shape((2 * HQ, HD), queries.dtype), [VMEM] * 2, queries, peer_queries, name="heads")
    slots, page_len, width = kv_pool.shape
    rows = slots * page_len
    cache, bias = kernel_call(
        pages_kernel,
        (shape((rows, width), kv_pool.dtype), shape((8, rows), jnp.float32)),
        [SMEM, SMEM, VMEM, VMEM], page_ids, cached_lengths, kv_pool, peer_pool, name="pages",
    )
    mask = 2
    received = swapped(gathered, "ctx", mask)
    while 2 * mask < devices:
        gathered = kernel_call(join_kernel, shape((2 * gathered.shape[0], HD), queries.dtype), [VMEM] * 2, gathered, received, name="join")
        mask *= 2
        received = swapped(gathered, "ctx", mask)
    states = kernel_call(
        attend_kernel, shape((devices, STATE_ROWS, HD), jnp.float32), [VMEM] * 5, gathered, received, cache, bias, new_kv, name="attend",
    )
    parts = lax.all_to_all(states, "ctx", split_axis=0, concat_axis=0, tiled=True)
    return kernel_call(settle_kernel, shape(queries.shape, queries.dtype), [VMEM], parts, name="settle")


def solution(mesh):
    placed = (
        P(("groups", "sess"), "ctx", None),
        P(("groups", "sess"), "ctx", None),
        P(("groups", "sess", "ctx"), None, None),
        P("groups", "ctx", None),
        P("groups"),
    )
    return jax.shard_map(body, mesh=mesh, in_specs=placed, out_specs=P(("groups", "sess"), "ctx", None), check_vma=False)
```

```python
import functools

import jax
import jax.numpy as jnp
from jax import lax
from jax.experimental import pallas as pl
from jax.experimental.pallas import tpu as pltpu
from jax.sharding import PartitionSpec as P

KVH = 4
HD = 128
GROUP = 8
HQ = KVH * GROUP
STATE_ROWS = HQ + GROUP
masked_value = -1e30
GRANT = 2**24
VMEM = pltpu.VMEM
SMEM = pltpu.SMEM


def swapped(value, axis, mask):
    pairs = [(source, source ^ mask) for source in range(lax.axis_size(axis))]
    return lax.ppermute(value, axis, pairs)


def spread_kernel(row_ref, out_ref):
    row = row_ref[0].astype(jnp.float32).reshape(HQ, HD).astype(out_ref.dtype)
    for place in range(out_ref.shape[0]):
        out_ref[place] = row


def pages_kernel(ids_ref, lengths_ref, pool_ref, peer_ref, cache_ref, bias_ref):
    session = lax.axis_index("sess")
    column = lax.axis_index("ctx")
    slots, page_len, _ = pool_ref.shape
    for slot in range(slots):
        ident = ids_ref[session, 0, slot]
        mine = (ident // slots) == session
        page = ident % slots
        cache_ref[slot * page_len : (slot + 1) * page_len, :] = jnp.where(
            mine, pool_ref[page], peer_ref[page]
        )
    rows = slots * page_len
    place = lax.broadcasted_iota(jnp.int32, bias_ref.shape, 1)
    left = lengths_ref[session] - column * rows
    bias_ref[...] = jnp.where(place < left, 0.0, masked_value)


def attend_kernel(turn, queries_ref, cache_ref, bias_ref, new_ref, out_ref):
    column = lax.axis_index("ctx")
    tokens = queries_ref.shape[0]
    queries = queries_ref[...].astype(jnp.float32)
    bias = bias_ref[0:1, :]
    fresh = new_ref[0].astype(jnp.float32)
    row = lax.broadcasted_iota(jnp.int32, (tokens * GROUP, 1), 0)
    fresh_bias = jnp.where((row // GROUP + turn) % tokens >= column, 0.0, masked_value)
    lane = lax.broadcasted_iota(jnp.int32, (tokens * GROUP, HD), 1)
    states = jnp.zeros((tokens * GROUP, HD), jnp.float32)
    for head in range(KVH):
        at = slice(head * HD, (head + 1) * HD)
        value_at = slice((KVH + head) * HD, (KVH + head + 1) * HD)
        query = queries[:, head * GROUP : (head + 1) * GROUP, :].reshape(tokens * GROUP, HD)
        scores = lax.dot_general(
            query.astype(jnp.bfloat16), cache_ref[:, at], (((1,), (1,)), ((), ())),
            preferred_element_type=jnp.float32,
        )
        scores = scores * HD ** (-0.5) + bias
        fresh_scores = jnp.sum(query * fresh[:, at], axis=1, keepdims=True) * HD ** (-0.5) + fresh_bias
        top = jnp.maximum(jnp.max(scores, axis=1, keepdims=True), fresh_scores)
        weights = jnp.exp(scores - top)
        fresh_weights = jnp.exp(fresh_scores - top)
        total = jnp.sum(weights, axis=1, keepdims=True) + fresh_weights
        coarse = weights.astype(jnp.bfloat16)
        fine = (weights - coarse.astype(jnp.float32)).astype(jnp.bfloat16)
        values = cache_ref[:, value_at]
        summed = (
            jnp.dot(coarse, values, preferred_element_type=jnp.float32)
            + jnp.dot(fine, values, preferred_element_type=jnp.float32)
            + fresh_weights * fresh[:, value_at]
        )
        states = jnp.where(lane == head, top, states)
        states = jnp.where(lane == KVH + head, total, states)
        out_ref[:, head * GROUP : (head + 1) * GROUP, :] = summed.reshape(tokens, GROUP, HD)
    out_ref[:, HQ:, :] = states.reshape(tokens, GROUP, HD)


def settle_kernel(parts_ref, out_ref):
    devices = parts_ref.shape[0]
    tops = [parts_ref[source, HQ:, :] for source in range(devices)]
    highest = functools.reduce(jnp.maximum, tops)
    weight_sum = 0.0
    factors = []
    for states in tops:
        factor = jnp.exp(states - highest)
        factors.append(factor)
        weight_sum = weight_sum + pltpu.roll(states, HD - KVH, 1) * factor
    pieces = []
    for head in range(KVH):
        summed = 0.0
        for source in range(devices):
            summed = summed + parts_ref[source, head * GROUP : (head + 1) * GROUP, :] * factors[source][:, head : head + 1]
        pieces.append(summed / weight_sum[:, head : head + 1])
    result = jnp.concatenate(pieces, axis=0)
    out_ref[0] = result.reshape(1, HQ * HD).astype(out_ref.dtype)


def kernel_call(kernel, out_shape, in_spaces, *operands, name=None):
    shapes = out_shape if isinstance(out_shape, (tuple, list)) else (out_shape,)
    specs = [pl.BlockSpec(memory_space=VMEM) for _ in shapes]
    return pl.pallas_call(
        kernel,
        out_shape=out_shape,
        in_specs=[pl.BlockSpec(memory_space=space) for space in in_spaces],
        out_specs=specs if isinstance(out_shape, (tuple, list)) else specs[0],
        name=name,
        compiler_params=pltpu.CompilerParams(vmem_limit_bytes=GRANT),
    )(*operands)


def exchanged(value, turn):
    devices = lax.axis_size("ctx")
    order = [(place + turn) % devices for place in range(devices)]
    return lax.all_to_all(value, "ctx", split_axis=0, concat_axis=0, axis_index_groups=[order], tiled=True)


def body(queries, new_kv, kv_pool, page_ids, cached_lengths):
    devices = lax.axis_size("ctx")
    turn = devices // 2
    shape = jax.ShapeDtypeStruct
    peer_pool = swapped(kv_pool, "sess", 1)
    spread = kernel_call(spread_kernel, shape((devices, HQ, HD), queries.dtype), [VMEM], queries, name="spread")
    gathered = exchanged(spread, turn)
    slots, page_len, width = kv_pool.shape
    rows = slots * page_len
    cache, bias = kernel_call(
        pages_kernel,
        (shape((rows, width), kv_pool.dtype), shape((8, rows), jnp.float32)),
        [SMEM, SMEM, VMEM, VMEM], page_ids, cached_lengths, kv_pool, peer_pool, name="pages",
    )
    states = kernel_call(
        functools.partial(attend_kernel, turn), shape((devices, STATE_ROWS, HD), jnp.float32), [VMEM] * 4, gathered, cache, bias, new_kv, name="attend",
    )
    parts = exchanged(states, turn)
    return kernel_call(settle_kernel, shape(queries.shape, queries.dtype), [VMEM], parts, name="settle")


def solution(mesh):
    placed = (
        P(("groups", "sess"), "ctx", None),
        P(("groups", "sess"), "ctx", None),
        P(("groups", "sess", "ctx"), None, None),
        P("groups", "ctx", None),
        P("groups"),
    )
    return jax.shard_map(body, mesh=mesh, in_specs=placed, out_specs=P(("groups", "sess"), "ctx", None), check_vma=False)
```

```python
import functools

import jax
import jax.numpy as jnp
from jax import lax
from jax.experimental import pallas as pl
from jax.experimental.pallas import tpu as pltpu
from jax.sharding import PartitionSpec as P

KVH = 4
HD = 128
GROUP = 8
HQ = KVH * GROUP
STATE_ROWS = HQ + GROUP
masked_value = -1e30
GRANT = 2**24
VMEM = pltpu.VMEM
SMEM = pltpu.SMEM


def swapped(value, axis, mask):
    pairs = [(source, source ^ mask) for source in range(lax.axis_size(axis))]
    return lax.ppermute(value, axis, pairs)


def prepare_kernel(
    row_hbm, new_hbm, pool_hbm, ids_hbm, lengths_hbm, out_ref, new_ref, pool_ref, bias_ref, pick_ref, row_ref, fresh_ref, ids_ref, lengths_ref, sems
):
    slots, page_len, _ = pool_ref.shape
    moves = [(row_hbm, row_ref), (ids_hbm, ids_ref), (lengths_hbm, lengths_ref), (new_hbm, fresh_ref), (pool_hbm, pool_ref)]
    copies = [pltpu.make_async_copy(source, target, sems.at[place]) for place, (source, target) in enumerate(moves)]
    for copy in copies:
        copy.start()
    session = lax.axis_index("sess")
    column = lax.axis_index("ctx")
    copies[0].wait()
    row = row_ref[0].astype(jnp.float32).reshape(HQ, HD).astype(out_ref.dtype)
    for place in range(out_ref.shape[0]):
        out_ref[place] = row
    copies[1].wait()
    copies[2].wait()
    left = lengths_ref[session] - column * slots * page_len
    lane = lax.broadcasted_iota(jnp.int32, bias_ref.shape, 1)
    bias_ref[...] = jnp.where(lane < left, 0.0, masked_value)
    for slot in range(slots):
        ident = ids_ref[session, 0, slot]
        physical = (ident // slots ^ session) * slots + ident % slots
        for page in range(1, 2 * slots):
            pick_ref[slot, page] = jnp.full(pick_ref.shape[2:], jnp.where(physical == page, 1.0, 0.0), jnp.float32).astype(pick_ref.dtype)
    copies[3].wait()
    new_ref[...] = fresh_ref[0].astype(jnp.float32).reshape(2 * KVH, HD)
    copies[4].wait()


def attend_kernel(first, second, queries_ref, pool_ref, peer_ref, bias_ref, pick_ref, new_ref, out_ref):
    column = lax.axis_index("ctx")
    tokens = queries_ref.shape[0]
    queries = queries_ref[...].astype(jnp.float32)
    bias = bias_ref[0:1, :]
    slots, page_len, _ = pool_ref.shape
    picked = [[None] + [jnp.concatenate([pick_ref[slot, page]] * (page_len // 16)) != 0 for page in range(1, 2 * slots)] for slot in range(slots)]
    row = lax.broadcasted_iota(jnp.int32, (tokens * GROUP, 1), 0)
    token = row // GROUP
    for place, value in enumerate(first):
        token = jnp.where(row // GROUP == place, value, token)
    fresh_bias = jnp.where(token >= column, 0.0, masked_value)
    pages = [(ref, page) for ref in (pool_ref, peer_ref) for page in range(ref.shape[0])]

    def chosen(slot, where):
        value = pages[0][0][pages[0][1], :, where]
        for mask, (ref, page) in zip(picked[slot][1:], pages[1:]):
            value = jnp.where(mask, ref[page, :, where], value)
        return value

    lane = lax.broadcasted_iota(jnp.int32, (tokens * GROUP, HD), 1)
    states = jnp.zeros((tokens * GROUP, HD), jnp.float32)
    for head in range(KVH):
        at = slice(head * HD, (head + 1) * HD)
        value_at = slice((KVH + head) * HD, (KVH + head + 1) * HD)
        query = queries[:, head * GROUP : (head + 1) * GROUP, :].reshape(tokens * GROUP, HD)
        keys, values = (jnp.concatenate([chosen(slot, where) for slot in range(slots)], axis=0) for where in (at, value_at))
        scores = lax.dot_general(
            query.astype(jnp.bfloat16), keys, (((1,), (1,)), ((), ())), preferred_element_type=jnp.float32
        )
        scores = scores * HD ** (-0.5) + bias
        fresh_scores = jnp.sum(query * new_ref[head : head + 1, :], axis=1, keepdims=True) * HD ** (-0.5) + fresh_bias
        top = jnp.maximum(jnp.max(scores, axis=1, keepdims=True), fresh_scores)
        weights = jnp.exp(scores - top)
        fresh_weights = jnp.exp(fresh_scores - top)
        total = jnp.sum(weights, axis=1, keepdims=True) + fresh_weights
        coarse = weights.astype(jnp.bfloat16)
        fine = (weights - coarse.astype(jnp.float32)).astype(jnp.bfloat16)
        summed = (
            jnp.dot(coarse, values, preferred_element_type=jnp.float32)
            + jnp.dot(fine, values, preferred_element_type=jnp.float32)
            + fresh_weights * new_ref[KVH + head : KVH + head + 1, :]
        )
        states = jnp.where(lane == head, top, states)
        states = jnp.where(lane == KVH + head, total, states)
        for place, value in enumerate(first):
            out_ref[second.index(value), head * GROUP : (head + 1) * GROUP, :] = summed[place * GROUP : (place + 1) * GROUP]
    for place, value in enumerate(first):
        out_ref[second.index(value), HQ:, :] = states[place * GROUP : (place + 1) * GROUP]


def settle_kernel(parts_ref, out_ref):
    devices = parts_ref.shape[0]
    tops = [parts_ref[source, HQ:, :] for source in range(devices)]
    highest = functools.reduce(jnp.maximum, tops)
    weight_sum = 0.0
    factors = []
    for states in tops:
        factor = jnp.exp(states - highest)
        factors.append(factor)
        weight_sum = weight_sum + pltpu.roll(states, HD - KVH, 1) * factor
    pieces = []
    for head in range(KVH):
        summed = 0.0
        for source in range(devices):
            summed = summed + parts_ref[source, head * GROUP : (head + 1) * GROUP, :] * factors[source][:, head : head + 1]
        pieces.append(summed / weight_sum[:, head : head + 1])
    result = jnp.concatenate(pieces, axis=0)
    out_ref[0] = result.reshape(1, HQ * HD).astype(out_ref.dtype)


def kernel_call(kernel, out_shape, *operands, name, space=VMEM, scratch=()):
    return pl.pallas_call(
        kernel,
        out_shape=out_shape,
        in_specs=[pl.BlockSpec(memory_space=space) for _ in operands],
        out_specs=jax.tree.map(lambda _: pl.BlockSpec(memory_space=VMEM), out_shape),
        scratch_shapes=scratch,
        name=name,
        compiler_params=pltpu.CompilerParams(vmem_limit_bytes=GRANT),
    )(*operands)


def exchanged(value, order):
    return lax.all_to_all(value, "ctx", split_axis=0, concat_axis=0, axis_index_groups=[order], tiled=True)


def body(queries, new_kv, kv_pool, page_ids, cached_lengths):
    devices = lax.axis_size("ctx")
    first = second = [(devices // 2 + 1 - place) % devices for place in range(devices)]
    shape = jax.ShapeDtypeStruct
    peer_pool = swapped(kv_pool, "sess", 1)
    slots, page_len, width = kv_pool.shape
    spread, fresh, pool, bias, pick = kernel_call(
        prepare_kernel,
        (
            shape((devices, HQ, HD), queries.dtype),
            shape((2 * KVH, HD), jnp.float32),
            shape(kv_pool.shape, kv_pool.dtype),
            shape((8, slots * page_len), jnp.float32),
            shape((slots, 2 * slots, 16, HD), kv_pool.dtype),
        ),
        *(pltpu.with_memory_space_constraint(value, pltpu.HBM) for value in (queries, new_kv, kv_pool, page_ids, cached_lengths)), name="prepare", space=pltpu.HBM,
        scratch=[
            VMEM(queries.shape, queries.dtype), VMEM(new_kv.shape, new_kv.dtype), SMEM(page_ids.shape, jnp.int32),
            SMEM(cached_lengths.shape, jnp.int32), pltpu.SemaphoreType.DMA((5,)),
        ],
    )
    gathered = exchanged(spread, first)
    states = kernel_call(
        functools.partial(attend_kernel, first, second), shape((devices, STATE_ROWS, HD), jnp.float32),
        gathered, pool, peer_pool, bias, pick, fresh, name="attend",
    )
    parts = exchanged(states, second)
    return kernel_call(settle_kernel, shape(queries.shape, queries.dtype), parts, name="settle")


def solution(mesh):
    placed = (
        P(("groups", "sess"), "ctx", None),
        P(("groups", "sess"), "ctx", None),
        P(("groups", "sess", "ctx"), None, None),
        P("groups", "ctx", None),
        P("groups"),
    )
    return jax.shard_map(body, mesh=mesh, in_specs=placed, out_specs=P(("groups", "sess"), "ctx", None), check_vma=False)
```

```python
import functools

import jax
import jax.numpy as jnp
from jax import lax
from jax.experimental import pallas as pl
from jax.experimental.pallas import tpu as pltpu
from jax.sharding import PartitionSpec as P

KVH = 4
HD = 128
GROUP = 8
HQ = KVH * GROUP
STATE_ROWS = HQ + GROUP
masked_value = -1e30
GRANT = 2**24
VMEM = pltpu.VMEM
SMEM = pltpu.SMEM


def swapped(value, axis, mask):
    pairs = [(source, source ^ mask) for source in range(lax.axis_size(axis))]
    return lax.ppermute(value, axis, pairs)


def prepare_kernel(
    row_hbm, new_hbm, pool_hbm, ids_hbm, lengths_hbm, out_ref, new_ref, pool_ref, bias_ref, pick_ref, row_ref, fresh_ref, ids_ref, lengths_ref, sems
):
    slots, page_len, _ = pool_ref.shape
    moves = [(row_hbm, row_ref), (ids_hbm, ids_ref), (lengths_hbm, lengths_ref), (new_hbm, fresh_ref), (pool_hbm, pool_ref)]
    copies = [pltpu.make_async_copy(source, target, sems.at[place]) for place, (source, target) in enumerate(moves)]
    for copy in copies:
        copy.start()
    session = lax.axis_index("sess")
    column = lax.axis_index("ctx")
    copies[0].wait()
    row = row_ref[0].astype(jnp.float32).reshape(HQ, HD).astype(out_ref.dtype)
    for place in range(out_ref.shape[0]):
        out_ref[place] = row
    copies[1].wait()
    copies[2].wait()
    left = lengths_ref[session] - column * slots * page_len
    lane = lax.broadcasted_iota(jnp.int32, (bias_ref.shape[0], page_len), 1)
    idents = [ids_ref[session, 0, slot] for slot in range(slots)]
    places = [(ident // slots ^ session) * slots + ident % slots for ident in idents]
    ranks = [sum((other < place).astype(jnp.int32) for other in places) for place in places]
    for block in range(slots):
        picked, start = jnp.int32(0), jnp.int32(0)
        for slot in range(slots):
            picked = jnp.where(ranks[slot] == block, places[slot], picked)
            start = jnp.where(ranks[slot] == block, slot * page_len, start)
        bias_ref[:, block * page_len : (block + 1) * page_len] = jnp.where(lane < left - start, 0.0, masked_value)
        for later in range(slots):
            flag = jnp.where(picked == block + 1 + later, 1.0, 0.0)
            pick_ref[block, later] = jnp.full(pick_ref.shape[2:], flag, jnp.float32).astype(pick_ref.dtype)
    copies[3].wait()
    new_ref[...] = fresh_ref[0].astype(jnp.float32).reshape(2 * KVH, HD)
    copies[4].wait()


def attend_kernel(order, queries_ref, pool_ref, peer_ref, bias_ref, pick_ref, new_ref, out_ref):
    column = lax.axis_index("ctx")
    tokens = queries_ref.shape[0]
    queries = queries_ref[...].astype(jnp.float32)
    bias = bias_ref[0:1, :]
    slots, page_len, _ = pool_ref.shape
    picked = [[jnp.concatenate([pick_ref[block, later]] * (page_len // 16)) != 0 for later in range(slots)] for block in range(slots)]
    row = lax.broadcasted_iota(jnp.int32, (tokens * GROUP, 1), 0)
    token = row // GROUP
    for place, value in enumerate(order):
        token = jnp.where(row // GROUP == place, value, token)
    fresh_bias = jnp.where(token >= column, 0.0, masked_value)
    pages = [(ref, page) for ref in (pool_ref, peer_ref) for page in range(ref.shape[0])]

    def chosen(where):
        loaded = [ref[page, :, where] for ref, page in pages]
        blocks = []
        for block in range(slots):
            value = loaded[block]
            for later, mask in enumerate(picked[block]):
                value = jnp.where(mask, loaded[block + 1 + later], value)
            blocks.append(value)
        return jnp.concatenate(blocks, axis=0)

    lane = lax.broadcasted_iota(jnp.int32, (tokens * GROUP, HD), 1)
    states = jnp.zeros((tokens * GROUP, HD), jnp.float32)
    columns = [slice(place * HD, (place + 1) * HD) for place in range(2 * KVH)]
    for heads in ((0, 1, 2, 3),):
        found = []
        for head in heads:
            query = queries[:, head * GROUP : (head + 1) * GROUP, :].reshape(tokens * GROUP, HD)
            scores = lax.dot_general(
                query.astype(jnp.bfloat16), chosen(columns[head]), (((1,), (1,)), ((), ())), preferred_element_type=jnp.float32
            )
            scores = scores * HD ** (-0.5) + bias
            fresh_scores = jnp.sum(query * new_ref[head : head + 1, :], axis=1, keepdims=True) * HD ** (-0.5) + fresh_bias
            found.append((scores, fresh_scores))
        tops = [jnp.maximum(jnp.max(scores, axis=1, keepdims=True), fresh_scores) for scores, fresh_scores in found]
        for head, (scores, fresh_scores), top in zip(heads, found, tops):
            weights = jnp.exp(scores - top)
            fresh_weights = jnp.exp(fresh_scores - top)
            total = jnp.sum(weights, axis=1, keepdims=True) + fresh_weights
            coarse = weights.astype(jnp.bfloat16)
            fine = (weights - coarse.astype(jnp.float32)).astype(jnp.bfloat16)
            values = chosen(columns[KVH + head])
            summed = (
                jnp.dot(coarse, values, preferred_element_type=jnp.float32)
                + jnp.dot(fine, values, preferred_element_type=jnp.float32)
                + fresh_weights * new_ref[KVH + head : KVH + head + 1, :]
            )
            states = jnp.where(lane == head, top, states)
            states = jnp.where(lane == KVH + head, total, states)
            out_ref[:, head * GROUP : (head + 1) * GROUP, :] = summed.reshape(tokens, GROUP, HD)
    out_ref[:, HQ:, :] = states.reshape(tokens, GROUP, HD)


def settle_kernel(parts_ref, out_ref):
    devices = parts_ref.shape[0]
    tops = [parts_ref[source, HQ:, :] for source in range(devices)]
    highest = functools.reduce(jnp.maximum, tops)
    weight_sum = 0.0
    factors = []
    for states in tops:
        factor = jnp.exp(states - highest)
        factors.append(factor)
        weight_sum = weight_sum + pltpu.roll(states, HD - KVH, 1) * factor
    pieces = []
    for head in range(KVH):
        summed = 0.0
        for source in range(devices):
            summed = summed + parts_ref[source, head * GROUP : (head + 1) * GROUP, :] * factors[source][:, head : head + 1]
        pieces.append(summed / weight_sum[:, head : head + 1])
    result = jnp.concatenate(pieces, axis=0)
    out_ref[0] = result.reshape(1, HQ * HD).astype(out_ref.dtype)


def kernel_call(kernel, out_shape, *operands, name, space=VMEM, scratch=()):
    return pl.pallas_call(
        kernel,
        out_shape=out_shape,
        in_specs=[pl.BlockSpec(memory_space=space) for _ in operands],
        out_specs=jax.tree.map(lambda _: pl.BlockSpec(memory_space=VMEM), out_shape),
        scratch_shapes=scratch,
        name=name,
        compiler_params=pltpu.CompilerParams(vmem_limit_bytes=GRANT),
    )(*operands)


def exchanged(value, order):
    return lax.all_to_all(value, "ctx", split_axis=0, concat_axis=0, axis_index_groups=[order], tiled=True)


def body(queries, new_kv, kv_pool, page_ids, cached_lengths):
    devices = lax.axis_size("ctx")
    order = [(devices // 2 + 1 - place) % devices for place in range(devices)]
    shape = jax.ShapeDtypeStruct
    peer_pool = swapped(kv_pool, "sess", 1)
    slots, page_len, width = kv_pool.shape
    spread, fresh, pool, bias, pick = kernel_call(
        prepare_kernel,
        (
            shape((devices, HQ, HD), queries.dtype),
            shape((2 * KVH, HD), jnp.float32),
            shape(kv_pool.shape, kv_pool.dtype),
            shape((8, slots * page_len), jnp.float32),
            shape((slots, slots, 16, HD), kv_pool.dtype),
        ),
        *(pltpu.with_memory_space_constraint(value, pltpu.HBM) for value in (queries, new_kv, kv_pool, page_ids, cached_lengths)), name="prepare", space=pltpu.HBM,
        scratch=[
            VMEM(queries.shape, queries.dtype), VMEM(new_kv.shape, new_kv.dtype), SMEM(page_ids.shape, jnp.int32),
            SMEM(cached_lengths.shape, jnp.int32), pltpu.SemaphoreType.DMA((5,)),
        ],
    )
    gathered = exchanged(spread, order)
    states = kernel_call(
        functools.partial(attend_kernel, order), shape((devices, STATE_ROWS, HD), jnp.float32),
        gathered, pool, peer_pool, bias, pick, fresh, name="attend",
    )
    parts = exchanged(states, order)
    return kernel_call(settle_kernel, shape(queries.shape, queries.dtype), parts, name="settle")


def solution(mesh):
    placed = (
        P(("groups", "sess"), "ctx", None),
        P(("groups", "sess"), "ctx", None),
        P(("groups", "sess", "ctx"), None, None),
        P("groups", "ctx", None),
        P("groups"),
    )
    return jax.shard_map(body, mesh=mesh, in_specs=placed, out_specs=P(("groups", "sess"), "ctx", None), check_vma=False)
```

```python
import functools

import jax
import jax.numpy as jnp
from jax import lax
from jax.experimental import pallas as pl
from jax.experimental.pallas import tpu as pltpu
from jax.sharding import PartitionSpec as P

KVH = 4
HD = 128
GROUP = 8
HQ = KVH * GROUP
STATE_ROWS = HQ + GROUP
masked_value = -1e30
GRANT = 2**24
VMEM = pltpu.VMEM
SMEM = pltpu.SMEM


def swapped(value, axis, mask):
    pairs = [(source, source ^ mask) for source in range(lax.axis_size(axis))]
    return lax.ppermute(value, axis, pairs)


def prepare_kernel(
    row_hbm, new_hbm, pool_hbm, ids_hbm, lengths_hbm, out_ref, new_ref, pool_ref, bias_ref, pick_ref, row_ref, fresh_ref, ids_ref, lengths_ref, sems
):
    slots, page_len, _ = pool_ref.shape
    moves = [(row_hbm, row_ref), (ids_hbm, ids_ref), (lengths_hbm, lengths_ref), (new_hbm, fresh_ref), (pool_hbm, pool_ref)]
    copies = [pltpu.make_async_copy(source, target, sems.at[place]) for place, (source, target) in enumerate(moves)]
    for copy in copies[::-1]:
        copy.start()
    session = lax.axis_index("sess")
    column = lax.axis_index("ctx")
    copies[0].wait()
    row = row_ref[0].astype(jnp.float32).reshape(HQ, HD).astype(out_ref.dtype)
    for place in range(out_ref.shape[0]):
        out_ref[place] = row
    copies[1].wait()
    copies[2].wait()
    left = lengths_ref[session] - column * slots * page_len
    lane = lax.broadcasted_iota(jnp.int32, (bias_ref.shape[0], page_len), 1)
    idents = [ids_ref[session, 0, slot] for slot in range(slots)]
    places = [(ident // slots ^ session) * slots + ident % slots for ident in idents]
    ranks = [sum((other < place).astype(jnp.int32) for other in places) for place in places]
    for block in range(slots):
        picked, start = jnp.int32(0), jnp.int32(0)
        for slot in range(slots):
            picked = jnp.where(ranks[slot] == block, places[slot], picked)
            start = jnp.where(ranks[slot] == block, slot * page_len, start)
        bias_ref[:, block * page_len : (block + 1) * page_len] = jnp.where(lane < left - start, 0.0, masked_value)
        for later in range(slots):
            flag = jnp.where(picked == block + 1 + later, 1.0, 0.0)
            pick_ref[block, later] = jnp.full(pick_ref.shape[2:], flag, jnp.float32).astype(pick_ref.dtype)
    copies[3].wait()
    new_ref[...] = fresh_ref[0].astype(jnp.float32).reshape(2 * KVH, HD)
    copies[4].wait()


def attend_kernel(order, queries_ref, pool_ref, peer_ref, bias_ref, pick_ref, new_ref, out_ref):
    column = lax.axis_index("ctx")
    tokens = queries_ref.shape[0]
    queries = queries_ref[...].astype(jnp.float32)
    bias = bias_ref[0:1, :]
    slots, page_len, _ = pool_ref.shape
    picked = [[jnp.concatenate([pick_ref[block, later]] * (page_len // 16)) != 0 for later in range(slots)] for block in range(slots)]
    row = lax.broadcasted_iota(jnp.int32, (tokens * GROUP, 1), 0)
    token = row // GROUP
    for place, value in enumerate(order):
        token = jnp.where(row // GROUP == place, value, token)
    fresh_bias = jnp.where(token >= column, 0.0, masked_value)
    pages = [(ref, page) for ref in (pool_ref, peer_ref) for page in range(ref.shape[0])]

    def chosen(where):
        loaded = [ref[page, :, where] for ref, page in pages]
        blocks = []
        for block in range(slots):
            value = loaded[block]
            for later, mask in enumerate(picked[block]):
                value = jnp.where(mask, loaded[block + 1 + later], value)
            blocks.append(value)
        return jnp.concatenate(blocks, axis=0)

    lane = lax.broadcasted_iota(jnp.int32, (tokens * GROUP, HD), 1)
    states = jnp.zeros((tokens * GROUP, HD), jnp.float32)
    columns = [slice(place * HD, (place + 1) * HD) for place in range(2 * KVH)]
    for heads in ((0, 1, 2, 3),):
        found = []
        for head in heads:
            query = queries[:, head * GROUP : (head + 1) * GROUP, :].reshape(tokens * GROUP, HD)
            scores = lax.dot_general(
                query.astype(jnp.bfloat16), chosen(columns[head]), (((1,), (1,)), ((), ())), preferred_element_type=jnp.float32
            )
            scores = scores * HD ** (-0.5) + bias
            fresh_scores = jnp.sum(query * new_ref[head : head + 1, :], axis=1, keepdims=True) * HD ** (-0.5) + fresh_bias
            found.append((scores, fresh_scores))
        tops = [jnp.maximum(jnp.max(scores, axis=1, keepdims=True), fresh_scores) for scores, fresh_scores in found]
        for head, (scores, fresh_scores), top in zip(heads, found, tops):
            weights = jnp.exp(scores - top)
            fresh_weights = jnp.exp(fresh_scores - top)
            total = jnp.sum(weights, axis=1, keepdims=True) + fresh_weights
            coarse = weights.astype(jnp.bfloat16)
            fine = (weights - coarse.astype(jnp.float32)).astype(jnp.bfloat16)
            values = chosen(columns[KVH + head])
            summed = (
                jnp.dot(coarse, values, preferred_element_type=jnp.float32)
                + jnp.dot(fine, values, preferred_element_type=jnp.float32)
                + fresh_weights * new_ref[KVH + head : KVH + head + 1, :]
            )
            states = jnp.where(lane == head, top, states)
            states = jnp.where(lane == KVH + head, total, states)
            out_ref[:, head * GROUP : (head + 1) * GROUP, :] = summed.reshape(tokens, GROUP, HD)
    out_ref[:, HQ:, :] = states.reshape(tokens, GROUP, HD)


def settle_kernel(parts_ref, out_ref):
    devices = parts_ref.shape[0]
    tops = [parts_ref[source, HQ:, :] for source in range(devices)]
    highest = functools.reduce(jnp.maximum, tops)
    weight_sum = 0.0
    factors = []
    for states in tops:
        factor = jnp.exp(states - highest)
        factors.append(factor)
        weight_sum = weight_sum + pltpu.roll(states, HD - KVH, 1) * factor
    pieces = []
    for head in range(KVH):
        summed = 0.0
        for source in range(devices):
            summed = summed + parts_ref[source, head * GROUP : (head + 1) * GROUP, :] * factors[source][:, head : head + 1]
        pieces.append(summed / weight_sum[:, head : head + 1])
    result = jnp.concatenate(pieces, axis=0)
    out_ref[0] = result.reshape(1, HQ * HD).astype(out_ref.dtype)


def kernel_call(kernel, out_shape, *operands, name, space=VMEM, scratch=()):
    return pl.pallas_call(
        kernel,
        out_shape=out_shape,
        in_specs=[pl.BlockSpec(memory_space=space) for _ in operands],
        out_specs=jax.tree.map(lambda _: pl.BlockSpec(memory_space=VMEM), out_shape),
        scratch_shapes=scratch,
        name=name,
        compiler_params=pltpu.CompilerParams(vmem_limit_bytes=GRANT),
    )(*operands)


def exchanged(value, order):
    return lax.all_to_all(value, "ctx", split_axis=0, concat_axis=0, axis_index_groups=[order], tiled=True)


def body(queries, new_kv, kv_pool, page_ids, cached_lengths):
    devices = lax.axis_size("ctx")
    order = [(devices // 2 + 1 - place) % devices for place in range(devices)]
    shape = jax.ShapeDtypeStruct
    peer_pool = swapped(kv_pool, "sess", 1)
    slots, page_len, width = kv_pool.shape
    spread, fresh, pool, bias, pick = kernel_call(
        prepare_kernel,
        (
            shape((devices, HQ, HD), queries.dtype),
            shape((2 * KVH, HD), jnp.float32),
            shape(kv_pool.shape, kv_pool.dtype),
            shape((8, slots * page_len), jnp.float32),
            shape((slots, slots, 16, HD), kv_pool.dtype),
        ),
        *(pltpu.with_memory_space_constraint(value, pltpu.HBM) for value in (queries, new_kv, kv_pool, page_ids, cached_lengths)), name="prepare", space=pltpu.HBM,
        scratch=[
            VMEM(queries.shape, queries.dtype), VMEM(new_kv.shape, new_kv.dtype), SMEM(page_ids.shape, jnp.int32),
            SMEM(cached_lengths.shape, jnp.int32), pltpu.SemaphoreType.DMA((5,)),
        ],
    )
    gathered = exchanged(spread, order)
    states = kernel_call(
        functools.partial(attend_kernel, order), shape((devices, STATE_ROWS, HD), jnp.float32),
        gathered, pool, peer_pool, bias, pick, fresh, name="attend",
    )
    parts = exchanged(states, order)
    return kernel_call(settle_kernel, shape(queries.shape, queries.dtype), parts, name="settle")


def solution(mesh):
    placed = (
        P(("groups", "sess"), "ctx", None),
        P(("groups", "sess"), "ctx", None),
        P(("groups", "sess", "ctx"), None, None),
        P("groups", "ctx", None),
        P("groups"),
    )
    return jax.shard_map(body, mesh=mesh, in_specs=placed, out_specs=P(("groups", "sess"), "ctx", None), check_vma=False)
```

```python
import functools

import jax
import jax.numpy as jnp
from jax import lax
from jax.experimental import pallas as pl
from jax.experimental.pallas import tpu as pltpu
from jax.sharding import PartitionSpec as P

KVH = 4
HD = 128
GROUP = 8
HQ = KVH * GROUP
STATE_ROWS = HQ + GROUP
masked_value = -30000.0
GRANT = 2**24
VMEM = pltpu.VMEM
SMEM = pltpu.SMEM


def swapped(value, axis, mask):
    pairs = [(source, source ^ mask) for source in range(lax.axis_size(axis))]
    return lax.ppermute(value, axis, pairs)


def prepare_kernel(
    row_hbm, new_hbm, pool_hbm, ids_hbm, lengths_hbm, out_ref, new_ref, pool_ref, bias_ref, pick_ref, row_ref, fresh_ref, ids_ref, lengths_ref, sems
):
    slots, page_len, _ = pool_ref.shape
    moves = [(row_hbm, row_ref), (ids_hbm, ids_ref), (lengths_hbm, lengths_ref), (new_hbm, fresh_ref), (pool_hbm, pool_ref)]
    copies = [pltpu.make_async_copy(source, target, sems.at[place]) for place, (source, target) in enumerate(moves)]
    for copy in copies[::-1]:
        copy.start()
    session = lax.axis_index("sess")
    column = lax.axis_index("ctx")
    copies[0].wait()
    row = row_ref[0].astype(jnp.float32).reshape(HQ, HD).astype(out_ref.dtype)
    for place in range(out_ref.shape[0]):
        out_ref[place] = row
    copies[1].wait()
    copies[2].wait()
    left = lengths_ref[session] - column * slots * page_len
    lane = lax.broadcasted_iota(jnp.int32, (bias_ref.shape[0], page_len), 1)
    idents = [ids_ref[session, 0, slot] for slot in range(slots)]
    places = [(ident // slots ^ session) * slots + ident % slots for ident in idents]
    ranks = [sum((other < place).astype(jnp.int32) for other in places) for place in places]
    for block in range(slots):
        picked, start = jnp.int32(0), jnp.int32(0)
        for slot in range(slots):
            picked = jnp.where(ranks[slot] == block, places[slot], picked)
            start = jnp.where(ranks[slot] == block, slot * page_len, start)
        bias_ref[:, block * page_len : (block + 1) * page_len] = jnp.where(lane < left - start, 0.0, masked_value)
        for later in range(slots):
            flag = jnp.where(picked == block + 1 + later, 1.0, 0.0)
            pick_ref[block, later] = jnp.full(pick_ref.shape[2:], flag, jnp.float32).astype(pick_ref.dtype)
    copies[3].wait()
    new_ref[...] = fresh_ref[0].astype(jnp.float32).reshape(2 * KVH, HD)
    copies[4].wait()


def pieces_of(value):
    parts = []
    for _ in range(2):
        scaled = value * 8193.0
        part = scaled - (scaled - value)
        parts.append(part)
        value = value - part
    return parts + [value]


def attend_kernel(order, queries_ref, pool_ref, peer_ref, bias_ref, pick_ref, new_ref, out_ref):
    column = lax.axis_index("ctx")
    tokens = queries_ref.shape[0]
    queries = queries_ref[...].astype(jnp.float32)
    bias = bias_ref[0:1, :]
    slots, page_len, _ = pool_ref.shape
    picked = [[jnp.concatenate([pick_ref[block, later]] * (page_len // 16)) != 0 for later in range(slots)] for block in range(slots)]
    row = lax.broadcasted_iota(jnp.int32, (tokens * GROUP, 1), 0)
    token = row // GROUP
    for place, value in enumerate(order):
        token = jnp.where(row // GROUP == place, value, token)
    fresh_bias = jnp.where(token >= column, 0.0, masked_value)
    pages = [(ref, page) for ref in (pool_ref, peer_ref) for page in range(ref.shape[0])]

    def chosen(where):
        loaded = [ref[page, :, where] for ref, page in pages]
        blocks = []
        for block in range(slots):
            value = loaded[block]
            for later, mask in enumerate(picked[block]):
                value = jnp.where(mask, loaded[block + 1 + later], value)
            blocks.append(value)
        return jnp.concatenate(blocks, axis=0)

    lane = lax.broadcasted_iota(jnp.int32, (tokens * GROUP, HD), 1)
    states = jnp.zeros((tokens * GROUP, HD), jnp.float32)
    columns = [slice(place * HD, (place + 1) * HD) for place in range(2 * KVH)]
    for heads in ((0, 1, 2, 3),):
        found = []
        for head in heads:
            query = queries[:, head * GROUP : (head + 1) * GROUP, :].reshape(tokens * GROUP, HD)
            scores = lax.dot_general(
                query.astype(jnp.bfloat16), chosen(columns[head]), (((1,), (1,)), ((), ())), preferred_element_type=jnp.float32
            )
            scores = scores * HD ** (-0.5) + bias
            fresh_scores = jnp.sum(query * new_ref[head : head + 1, :], axis=1, keepdims=True) * HD ** (-0.5) + fresh_bias
            found.append((scores, fresh_scores))
        tops = [jnp.maximum(jnp.max(scores, axis=1, keepdims=True), fresh_scores) for scores, fresh_scores in found]
        for head, (scores, fresh_scores), top in zip(heads, found, tops):
            weights = jnp.exp(scores - top)
            fresh_weights = jnp.exp(fresh_scores - top)
            total = jnp.sum(weights, axis=1, keepdims=True) + fresh_weights
            coarse = weights.astype(jnp.bfloat16)
            values = chosen(columns[KVH + head])
            summed = (
                jnp.dot(coarse, values, preferred_element_type=jnp.float32)
                + fresh_weights * new_ref[KVH + head : KVH + head + 1, :]
            )
            peak = jnp.maximum(jnp.max(jnp.abs(summed), axis=1, keepdims=True), 1e-30)
            summed = summed / peak
            for place, part in enumerate(pieces_of(top + jnp.log(total)) + pieces_of(jnp.log(peak / total))):
                states = jnp.where(lane == place * KVH + head, part, states)
            out_ref[:, head * GROUP : (head + 1) * GROUP, :] = summed.reshape(tokens, GROUP, HD)
    out_ref[:, HQ:, :] = states.reshape(tokens, GROUP, HD)


def settle_kernel(parts_ref, out_ref):
    devices = parts_ref.shape[0]
    found = [parts_ref[source, HQ:, :] for source in range(devices)]
    tops = [sum((pltpu.roll(states, HD - place * KVH, 1) for place in (1, 2)), states) for states in found]
    peaks = [sum(pltpu.roll(states, HD - place * KVH, 1) for place in (3, 4, 5)) for states in found]
    highest = functools.reduce(jnp.maximum, tops)
    weight_sum = 0.0
    factors = []
    for top, peak in zip(tops, peaks):
        factors.append(jnp.exp(top - highest + peak))
        weight_sum = weight_sum + jnp.exp(top - highest)
    pieces = []
    for head in range(KVH):
        summed = 0.0
        for source in range(devices):
            summed = summed + parts_ref[source, head * GROUP : (head + 1) * GROUP, :] * factors[source][:, head : head + 1]
        pieces.append(summed / weight_sum[:, head : head + 1])
    result = jnp.concatenate(pieces, axis=0)
    out_ref[0] = result.reshape(1, HQ * HD).astype(out_ref.dtype)


def kernel_call(kernel, out_shape, *operands, name, space=VMEM, scratch=()):
    return pl.pallas_call(
        kernel,
        out_shape=out_shape,
        in_specs=[pl.BlockSpec(memory_space=space) for _ in operands],
        out_specs=jax.tree.map(lambda _: pl.BlockSpec(memory_space=VMEM), out_shape),
        scratch_shapes=scratch,
        name=name,
        compiler_params=pltpu.CompilerParams(vmem_limit_bytes=GRANT),
    )(*operands)


def exchanged(value, order):
    return lax.all_to_all(value, "ctx", split_axis=0, concat_axis=0, axis_index_groups=[order], tiled=True)


def body(queries, new_kv, kv_pool, page_ids, cached_lengths):
    devices = lax.axis_size("ctx")
    order = [(devices // 2 + 1 - place) % devices for place in range(devices)]
    shape = jax.ShapeDtypeStruct
    peer_pool = swapped(kv_pool, "sess", 1)
    slots, page_len, width = kv_pool.shape
    spread, fresh, pool, bias, pick = kernel_call(
        prepare_kernel,
        (
            shape((devices, HQ, HD), queries.dtype),
            shape((2 * KVH, HD), jnp.float32),
            shape(kv_pool.shape, kv_pool.dtype),
            shape((8, slots * page_len), jnp.float32),
            shape((slots, slots, 16, HD), kv_pool.dtype),
        ),
        *(pltpu.with_memory_space_constraint(value, pltpu.HBM) for value in (queries, new_kv, kv_pool, page_ids, cached_lengths)), name="prepare", space=pltpu.HBM,
        scratch=[
            VMEM(queries.shape, queries.dtype), VMEM(new_kv.shape, new_kv.dtype), SMEM(page_ids.shape, jnp.int32),
            SMEM(cached_lengths.shape, jnp.int32), pltpu.SemaphoreType.DMA((5,)),
        ],
    )
    gathered = exchanged(spread, order)
    states = kernel_call(
        functools.partial(attend_kernel, order), shape((devices, STATE_ROWS, HD), jnp.float32),
        gathered, pool, peer_pool, bias, pick, fresh, name="attend",
    )
    parts = exchanged(states.astype(jnp.float16), order).astype(jnp.float32)
    return kernel_call(settle_kernel, shape(queries.shape, queries.dtype), parts, name="settle")


def solution(mesh):
    placed = (
        P(("groups", "sess"), "ctx", None),
        P(("groups", "sess"), "ctx", None),
        P(("groups", "sess", "ctx"), None, None),
        P("groups", "ctx", None),
        P("groups"),
    )
    return jax.shard_map(body, mesh=mesh, in_specs=placed, out_specs=P(("groups", "sess"), "ctx", None), check_vma=False)
```

```python
import functools

import jax
import jax.numpy as jnp
from jax import lax
from jax.experimental import pallas as pl
from jax.experimental.pallas import tpu as pltpu
from jax.sharding import PartitionSpec as P

KVH = 4
HD = 128
GROUP = 8
HQ = KVH * GROUP
STATE_ROWS = HQ + GROUP
masked_value = -1e30
GRANT = 2**24
VMEM = pltpu.VMEM
SMEM = pltpu.SMEM


def swapped(value, axis, mask):
    pairs = [(source, source ^ mask) for source in range(lax.axis_size(axis))]
    return lax.ppermute(value, axis, pairs)


def prepare_kernel(
    row_hbm, new_hbm, pool_hbm, ids_hbm, lengths_hbm, out_ref, new_ref, pool_ref, bias_ref, pick_ref, row_ref, fresh_ref, ids_ref, lengths_ref, sems
):
    slots, page_len, _ = pool_ref.shape
    moves = [(row_hbm, row_ref), (ids_hbm, ids_ref), (lengths_hbm, lengths_ref), (new_hbm, fresh_ref), (pool_hbm, pool_ref)]
    copies = [pltpu.make_async_copy(source, target, sems.at[place]) for place, (source, target) in enumerate(moves)]
    for copy in copies[::-1]:
        copy.start()
    session = lax.axis_index("sess")
    column = lax.axis_index("ctx")
    copies[0].wait()
    row = row_ref[0].astype(jnp.float32).reshape(HQ, HD).astype(out_ref.dtype)
    for place in range(out_ref.shape[0]):
        out_ref[place] = row
    copies[1].wait()
    copies[2].wait()
    left = lengths_ref[session] - column * slots * page_len
    lane = lax.broadcasted_iota(jnp.int32, (bias_ref.shape[0], page_len), 1)
    idents = [ids_ref[session, 0, slot] for slot in range(slots)]
    places = [(ident // slots ^ session) * slots + ident % slots for ident in idents]
    ranks = [sum((other < place).astype(jnp.int32) for other in places) for place in places]
    for block in range(slots):
        picked, start = jnp.int32(0), jnp.int32(0)
        for slot in range(slots):
            picked = jnp.where(ranks[slot] == block, places[slot], picked)
            start = jnp.where(ranks[slot] == block, slot * page_len, start)
        bias_ref[:, block * page_len : (block + 1) * page_len] = jnp.where(lane < left - start, 0.0, masked_value)
        for later in range(slots):
            flag = jnp.where(picked == block + 1 + later, 1.0, 0.0)
            pick_ref[block, later] = jnp.full(pick_ref.shape[2:], flag, jnp.float32).astype(pick_ref.dtype)
    copies[3].wait()
    new_ref[...] = fresh_ref[0].astype(jnp.float32).reshape(2 * KVH, HD)
    copies[4].wait()


def attend_kernel(order, queries_ref, pool_ref, peer_ref, bias_ref, pick_ref, new_ref, out_ref):
    column = lax.axis_index("ctx")
    tokens = queries_ref.shape[0]
    queries = queries_ref[...].astype(jnp.float32)
    bias = bias_ref[0:1, :]
    slots, page_len, _ = pool_ref.shape
    picked = [[jnp.concatenate([pick_ref[block, later]] * (page_len // 16)) != 0 for later in range(slots)] for block in range(slots)]
    row = lax.broadcasted_iota(jnp.int32, (tokens * GROUP, 1), 0)
    token = row // GROUP
    for place, value in enumerate(order):
        token = jnp.where(row // GROUP == place, value, token)
    fresh_bias = jnp.where(token >= column, 0.0, masked_value)
    pages = [(ref, page) for ref in (pool_ref, peer_ref) for page in range(ref.shape[0])]

    def chosen(where):
        loaded = [ref[page, :, where] for ref, page in pages]
        blocks = []
        for block in range(slots):
            value = loaded[block]
            for later, mask in enumerate(picked[block]):
                value = jnp.where(mask, loaded[block + 1 + later], value)
            blocks.append(value)
        return jnp.concatenate(blocks, axis=0)

    lane = lax.broadcasted_iota(jnp.int32, (tokens * GROUP, HD), 1)
    states = jnp.zeros((tokens * GROUP, HD), jnp.float32)
    columns = [slice(place * HD, (place + 1) * HD) for place in range(2 * KVH)]
    for heads in ((0, 1, 2, 3),):
        found = []
        for head in heads:
            query = queries[:, head * GROUP : (head + 1) * GROUP, :].reshape(tokens * GROUP, HD)
            scores = lax.dot_general(
                query.astype(jnp.bfloat16), chosen(columns[head]), (((1,), (1,)), ((), ())), preferred_element_type=jnp.float32
            )
            scores = scores * HD ** (-0.5) + bias
            fresh_scores = jnp.sum(query * new_ref[head : head + 1, :], axis=1, keepdims=True) * HD ** (-0.5) + fresh_bias
            found.append((scores, fresh_scores))
        tops = [jnp.maximum(jnp.max(scores, axis=1, keepdims=True), fresh_scores) for scores, fresh_scores in found]
        for head, (scores, fresh_scores), top in zip(heads, found, tops):
            coarse = jnp.exp(scores - top).astype(jnp.bfloat16)
            fresh_weights = jnp.exp(fresh_scores - top)
            values = chosen(columns[KVH + head])
            both = jnp.dot(coarse, jnp.concatenate([values, jnp.ones_like(values)], axis=1), preferred_element_type=jnp.float32)
            total = both[:, HD:] + fresh_weights
            summed = (
                both[:, :HD]
                + fresh_weights * new_ref[KVH + head : KVH + head + 1, :]
            )
            states = jnp.where(lane == head, top, states)
            states = jnp.where(lane == KVH + head, total, states)
            out_ref[:, head * GROUP : (head + 1) * GROUP, :] = summed.reshape(tokens, GROUP, HD)
    out_ref[:, HQ:, :] = states.reshape(tokens, GROUP, HD)


def settle_kernel(parts_ref, out_ref):
    devices = parts_ref.shape[0]
    tops = [parts_ref[source, HQ:, :] for source in range(devices)]
    highest = functools.reduce(jnp.maximum, tops)
    weight_sum = 0.0
    factors = []
    for states in tops:
        factor = jnp.exp(states - highest)
        factors.append(factor)
        weight_sum = weight_sum + pltpu.roll(states, HD - KVH, 1) * factor
    pieces = []
    for head in range(KVH):
        summed = 0.0
        for source in range(devices):
            summed = summed + parts_ref[source, head * GROUP : (head + 1) * GROUP, :] * factors[source][:, head : head + 1]
        pieces.append(summed / weight_sum[:, head : head + 1])
    result = jnp.concatenate(pieces, axis=0)
    out_ref[0] = result.reshape(1, HQ * HD).astype(out_ref.dtype)


def kernel_call(kernel, out_shape, *operands, name, space=VMEM, scratch=()):
    return pl.pallas_call(
        kernel,
        out_shape=out_shape,
        in_specs=[pl.BlockSpec(memory_space=space) for _ in operands],
        out_specs=jax.tree.map(lambda _: pl.BlockSpec(memory_space=VMEM), out_shape),
        scratch_shapes=scratch,
        name=name,
        compiler_params=pltpu.CompilerParams(vmem_limit_bytes=GRANT),
    )(*operands)


def exchanged(value, order):
    return lax.all_to_all(value, "ctx", split_axis=0, concat_axis=0, axis_index_groups=[order], tiled=True)


def body(queries, new_kv, kv_pool, page_ids, cached_lengths):
    devices = lax.axis_size("ctx")
    order = [(devices // 2 + 1 - place) % devices for place in range(devices)]
    shape = jax.ShapeDtypeStruct
    peer_pool = swapped(kv_pool, "sess", 1)
    slots, page_len, width = kv_pool.shape
    spread, fresh, pool, bias, pick = kernel_call(
        prepare_kernel,
        (
            shape((devices, HQ, HD), queries.dtype),
            shape((2 * KVH, HD), jnp.float32),
            shape(kv_pool.shape, kv_pool.dtype),
            shape((8, slots * page_len), jnp.float32),
            shape((slots, slots, 16, HD), kv_pool.dtype),
        ),
        *(pltpu.with_memory_space_constraint(value, pltpu.HBM) for value in (queries, new_kv, kv_pool, page_ids, cached_lengths)), name="prepare", space=pltpu.HBM,
        scratch=[
            VMEM(queries.shape, queries.dtype), VMEM(new_kv.shape, new_kv.dtype), SMEM(page_ids.shape, jnp.int32),
            SMEM(cached_lengths.shape, jnp.int32), pltpu.SemaphoreType.DMA((5,)),
        ],
    )
    gathered = exchanged(spread, order)
    states = kernel_call(
        functools.partial(attend_kernel, order), shape((devices, STATE_ROWS, HD), jnp.float32),
        gathered, pool, peer_pool, bias, pick, fresh, name="attend",
    )
    parts = exchanged(states, order)
    return kernel_call(settle_kernel, shape(queries.shape, queries.dtype), parts, name="settle")


def solution(mesh):
    placed = (
        P(("groups", "sess"), "ctx", None),
        P(("groups", "sess"), "ctx", None),
        P(("groups", "sess", "ctx"), None, None),
        P("groups", "ctx", None),
        P("groups"),
    )
    return jax.shard_map(body, mesh=mesh, in_specs=placed, out_specs=P(("groups", "sess"), "ctx", None), check_vma=False)
```
